32 devices in a mesh: dp: 16 (over z, y, x), ctx: 2 (over core).
Axes of the slice: x: 2, y: 2, z: 4, core: 2. Of those that a mesh axis runs over, the one named last changes fastest.
Arguments:
- inputs: float32 [16, 512, 768], P('dp', 'ctx'), may hold values from -6 to 6
- segments: int32 [16, 512], P('dp'), may hold values from 0 to 2, as said below
- norm_gain: float32 [768], P(('dp', 'ctx')), may hold values from 0.5 to 1.5
- in_weight: bfloat16 [768, 3352], P(('dp', 'ctx')), may hold values from -0.21875 to 0.21875
- conv_weight: float32 [1792, 4], P(('dp', 'ctx')), may hold values from -3 to 3
- conv_bias: float32 [1792], P(('dp', 'ctx')), may hold values from -3 to 3
- dt_bias: float32 [24], replicated, may hold values from -6 to -2
- a_log: float32 [24], replicated, may hold values from 0 to 2.5
- d_skip: float32 [24], replicated, may hold values from 0.5 to 1.5
- gate_gain: float32 [1536], P(('dp', 'ctx')), may hold values from 0.5 to 1.5
- out_weight: bfloat16 [1536, 768], P(('dp', 'ctx')), may hold values from -0.15625 to 0.15625
- cotangent: float32 [16, 512, 768], P('dp', 'ctx'), may hold values from -6 to 6
Outputs:
- output: float32 [16, 512, 768], P('dp', 'ctx')
- d_inputs: float32 [16, 512, 768], P('dp', 'ctx')
- d_norm_gain: float32 [768], P(('dp', 'ctx'))
- d_in_weight: float32 [768, 3352], P(('dp', 'ctx'))
- d_conv_weight: float32 [1792, 4], P(('dp', 'ctx'))
- d_conv_bias: float32 [1792], P(('dp', 'ctx'))
- d_dt_bias: float32 [24], replicated
- d_a_log: float32 [24], replicated
- d_d_skip: float32 [24], replicated
- d_gate_gain: float32 [1536], P(('dp', 'ctx'))
- d_out_weight: float32 [1536, 768], P(('dp', 'ctx'))
The draws below stay inside these ranges and needn't reach their ends.
Inputs may be any that keep to these rules, and one draw needn't show every extreme that they name: `segments`: in every sequence the numbers never fall and take each of 0, 1 and 2 on one run of positions; document 0 ends before position 256.
All inputs are finite; a program needn't handle non-finite values.
Results may differ from the reference program's by a relative error of at most 0.0093.
Values may be sent and summed in bfloat16 or wider, within the bound.
No kernel may reach another device: no remote copies, remote signals or barrier semaphores. Data moves between devices by JAX's collectives and lax.ppermute only.
A program may use at most 128 MiB of HBM per device.

```python
import math
import jax
import jax.numpy as jnp
from jax import lax

D = 768
HEADS = 24
HEADDIM = 64
NSTATE = 128
CONV = 4
INNER = 1536
CONVDIM = 1792
PROJ = 3352
LSEQ = 512
SEQS = 16


def draw_segments(key, part):
    first_key, second_key = jax.random.split(key)
    first = jax.random.randint(first_key, (SEQS, 1), LSEQ // 8, LSEQ // 2)
    second = first + jax.random.randint(second_key, (SEQS, 1), LSEQ // 4, LSEQ // 2)
    places = jnp.arange(LSEQ)[None, :]
    return (places >= first).astype(jnp.int32) + (places >= second).astype(jnp.int32)


def block_levels(key, extent, cuts, least, largest):
    def one(dim, blocks):
        steps = jax.random.uniform(jax.random.fold_in(jax.random.fold_in(key, 6), dim), (blocks,), jnp.float32, least / len(cuts), largest / len(cuts))
        return jnp.repeat(jnp.exp(steps), extent[dim] // blocks).reshape((-1,) + (1,) * (len(extent) - dim - 1))

    level = one(*cuts[0])
    for cut in cuts[1:]:
        level = level * one(*cut)
    return level


def bell_draw(key, dims, scale, most, cuts=(), kind=jnp.bfloat16):
    values = jax.random.normal(key, dims, jnp.float32) * scale
    if len(cuts) > 0:
        values = block_levels(key, dims, cuts, -0.22, 0.18) * values
    return jnp.clip(values, min=-most, max=most).astype(kind)


def setup_inputs(seed: int = 0) -> dict:
    key_of = jax.random.split(jax.random.key(seed), 13)
    inputs = bell_draw(key_of[0], (SEQS, LSEQ, D), 1.0, 6.0, ((0, 16), (1, 2)), jnp.float32)
    segments = draw_segments(jax.random.fold_in(key_of[12], 71), 0)
    norm_gain = jnp.clip(1.0 + 0.1 * jax.random.normal(key_of[2], (D,), jnp.float32), 0.5, 1.5)
    in_weight = bell_draw(key_of[3], (D, PROJ), D ** -0.5, 0.21875, ((0, 32),))
    conv_weight = bell_draw(key_of[4], (CONVDIM, CONV), CONV ** -0.5, 3.0, ((0, 32),), jnp.float32)
    conv_bias = bell_draw(key_of[5], (CONVDIM,), 0.5, 3.0, ((0, 32),), jnp.float32)
    dt_bias = jnp.clip(jax.random.uniform(key_of[6], (HEADS,), jnp.float32, -6.0, -2.0), -6.0, -2.0)
    a_log = jnp.clip(jax.random.uniform(key_of[7], (HEADS,), jnp.float32, 0.0, 2.5), 0.0, 2.5)
    d_skip = jnp.clip(jax.random.uniform(key_of[8], (HEADS,), jnp.float32, 0.5, 1.5), 0.5, 1.5)
    gate_gain = jnp.clip(1.0 + 0.1 * jax.random.normal(key_of[9], (INNER,), jnp.float32), 0.5, 1.5)
    out_weight = bell_draw(key_of[10], (INNER, D), INNER ** -0.5, 0.15625, ((0, 32),))
    cotangent = bell_draw(key_of[11], (SEQS, LSEQ, D), 1.0, 6.0, ((0, 16), (1, 2)), jnp.float32)
    return dict(inputs=inputs, segments=segments, norm_gain=norm_gain, in_weight=in_weight, conv_weight=conv_weight, conv_bias=conv_bias, dt_bias=dt_bias, a_log=a_log, d_skip=d_skip, gate_gain=gate_gain, out_weight=out_weight, cotangent=cotangent)


EPS = 1e-05
BEST = lax.Precision.HIGHEST

def prenorm(values, gain):
    return values * lax.rsqrt(lax.optimization_barrier(jnp.mean(values * values, axis=-1, keepdims=True)) + EPS) * gain

def conv_section(extended, seg_ext, conv_weight, conv_bias):
    taps = conv_weight.shape[1]
    length = extended.shape[1] - taps + 1
    own_seg = seg_ext[:, taps - 1:]
    total = conv_bias + jnp.zeros((extended.shape[0], length, extended.shape[2]), jnp.float32)
    for offset in range(taps):
        rows = extended[:, offset:offset + length]
        keep = (seg_ext[:, offset:offset + length] == own_seg)[..., None]
        total = total + jnp.where(keep, rows * conv_weight[:, offset], 0.0)
    return jax.nn.silu(total)

def prepare(projected, rim_rows, seg_ext, conv_weight, conv_bias, dt_bias, a_log):
    gate_part = projected[..., :INNER]
    conv_in = projected[..., INNER:INNER + CONVDIM]
    dt_raw = projected[..., INNER + CONVDIM:]
    extended = jnp.concatenate([rim_rows, conv_in], axis=1)
    convolved = conv_section(extended, seg_ext, conv_weight, conv_bias)
    values = convolved[..., :INNER]
    b_mat = convolved[..., INNER:INNER + NSTATE]
    c_mat = convolved[..., INNER + NSTATE:]
    step_size = jax.nn.softplus(dt_raw + dt_bias)
    log_decay = jnp.cumsum(-jnp.exp(a_log) * step_size, axis=1)
    return (gate_part, values, b_mat, c_mat, step_size, log_decay)

def finish(feats, d_skip, gate_gain, state_in, own_seg, seg_before):
    gate_part, values, b_mat, c_mat, step_size, log_decay = feats
    seq_count, length = own_seg.shape
    causal = jnp.arange(length)[:, None] >= jnp.arange(length)[None, :]
    mask = (own_seg[:, :, None] == own_seg[:, None, :]) & causal[None]
    by_head = jnp.swapaxes(log_decay, 1, 2)
    differ = by_head[:, :, :, None] - by_head[:, :, None, :]
    decay = jnp.exp(jnp.where(mask[:, None], differ, -1e+30))
    scores = jnp.einsum('stn,sun->stu', c_mat, b_mat, precision=BEST)
    weights = decay * scores[:, None]
    heads_vals = values.reshape(seq_count, length, HEADS, HEADDIM)
    scaled = heads_vals * step_size[..., None]
    mixed = jnp.einsum('shtu,suhp->sthp', weights, scaled, precision=BEST)
    carry_keep = jnp.where((own_seg == seg_before[:, None])[..., None], jnp.exp(log_decay), 0.0)
    mixed = mixed + jnp.einsum('stn,shpn->sthp', c_mat, state_in, precision=BEST) * carry_keep[..., None]
    mixed = mixed + d_skip[:, None] * heads_vals
    mixed = mixed.reshape(seq_count, length, INNER)
    gated = mixed * jax.nn.silu(gate_part)
    return gated * lax.rsqrt(lax.optimization_barrier(jnp.mean(gated * gated, axis=-1, keepdims=True)) + EPS) * gate_gain

def reference(inputs, segments, norm_gain, in_weight, conv_weight, conv_bias, dt_bias, a_log, d_skip, gate_gain, out_weight, cotangent):
    group = math.gcd(SEQS, 4)
    blocks = SEQS // group

    def one_block(totals, items):
        block_in, block_seg, block_cot = items
        normed, norm_pull = jax.vjp(prenorm, block_in, norm_gain)
        normed_bf = normed.astype(jnp.bfloat16).reshape(group * LSEQ, D)
        projected = jnp.dot(normed_bf, in_weight, preferred_element_type=jnp.float32).astype(jnp.bfloat16)
        proj_f = lax.optimization_barrier(projected).astype(jnp.float32).reshape(group, LSEQ, PROJ)
        rim_rows = jnp.zeros((group, CONV - 1, CONVDIM), jnp.float32)
        seg_ext = jnp.concatenate([jnp.repeat(block_seg[:, :1], CONV - 1, axis=1), block_seg], axis=1)
        state_zero = jnp.zeros((group, HEADS, HEADDIM, NSTATE), jnp.float32)

        def mixer(proj_in, weight_in, bias_in, dt_in, alog_in, skip_in, gain_in):
            feats = prepare(proj_in, rim_rows, seg_ext, weight_in, bias_in, dt_in, alog_in)
            return finish(feats, skip_in, gain_in, state_zero, block_seg, block_seg[:, 0])
        mixer_f, mixer_pull = jax.vjp(mixer, proj_f, conv_weight, conv_bias, dt_bias, a_log, d_skip, gate_gain)
        mixer_bf = mixer_f.astype(jnp.bfloat16).reshape(group * LSEQ, INNER)
        result = block_in + jnp.dot(mixer_bf, out_weight, preferred_element_type=jnp.float32).reshape(group, LSEQ, D)
        cot_bf = block_cot.astype(jnp.bfloat16).reshape(group * LSEQ, D)
        grad_out_w = jnp.dot(mixer_bf.T, cot_bf, preferred_element_type=jnp.float32)
        d_mixer = jnp.dot(cot_bf, out_weight.T, preferred_element_type=jnp.float32).reshape(group, LSEQ, INNER)
        grad_proj, grad_cw, grad_cb, grad_dt, grad_al, grad_ds, grad_gg = mixer_pull(d_mixer)
        grad_proj_bf = grad_proj.astype(jnp.bfloat16).reshape(group * LSEQ, PROJ)
        grad_in_w = jnp.dot(normed_bf.T, grad_proj_bf, preferred_element_type=jnp.float32)
        d_normed = jnp.dot(grad_proj_bf, in_weight.T, preferred_element_type=jnp.float32).reshape(group, LSEQ, D)
        grad_x, grad_ng = norm_pull(d_normed)
        grad_inputs = block_cot + grad_x
        parts = (grad_ng, grad_in_w, grad_cw, grad_cb, grad_dt, grad_al, grad_ds, grad_gg, grad_out_w)
        totals = tuple((total + part for total, part in zip(totals, parts)))
        return (totals, (result, grad_inputs))
    start = (jnp.zeros((D,), jnp.float32), jnp.zeros((D, PROJ), jnp.float32), jnp.zeros((CONVDIM, CONV), jnp.float32), jnp.zeros((CONVDIM,), jnp.float32), jnp.zeros((HEADS,), jnp.float32), jnp.zeros((HEADS,), jnp.float32), jnp.zeros((HEADS,), jnp.float32), jnp.zeros((INNER,), jnp.float32), jnp.zeros((INNER, D), jnp.float32))
    items = (inputs.reshape(blocks, group, LSEQ, D), segments.reshape(blocks, group, LSEQ), cotangent.reshape(blocks, group, LSEQ, D))
    totals, (results, grads) = lax.scan(one_block, start, items)
    output = results.reshape(SEQS, LSEQ, D)
    d_inputs = grads.reshape(SEQS, LSEQ, D)
    return (output, d_inputs, totals[0], totals[1], totals[2], totals[3], totals[4], totals[5], totals[6], totals[7], totals[8])
```

```python
import functools

import jax
import jax.numpy as jnp
from jax import lax
from jax.experimental import pallas as pl
from jax.experimental.pallas import tpu as pltpu
from jax.sharding import PartitionSpec as P

HEADS = 24
HEADDIM = 64
NSTATE = 128
CONV = 4
INNER = 1536
CONVDIM = 1792
EPS = 1e-05

LANES = 128
SLABS = 4
BLOCKS = 16
CHUNK = 128
BF = jnp.bfloat16
F32 = jnp.float32
BEST = lax.Precision.HIGHEST
ZOFF = (0, 8, 4, 12)

LOCAL = INNER // 2
PAIRS = LOCAL // LANES
XBC = LOCAL + 2 * NSTATE
COLS1 = XBC + LANES
TILES1 = COLS1 // LANES
TILES1A = 5
TILESZ = LOCAL // LANES


def offsets(first):
    return [ZOFF[n % 4] ^ (first if n >= 4 else 0) for n in range(8)]


OFF_A = offsets(1)
OFF_B = offsets(2)


def mm(a, b, dims=((1,), (0,)), precision=None):
    return lax.dot_general(
        a, b, (dims, ((), ())), preferred_element_type=F32, precision=precision
    )


def nt(a, b):
    return mm(a, b, ((1,), (1,)))


def tn(a, b):
    return mm(a, b, ((0,), (0,)))


def in_row(idx):
    return idx


def out_row(idx):
    low = idx & 3
    return (idx - low) + ((low & 1) * 2) + (low >> 1)


def each_block(me, offs, other, rows, row_of):
    for n in range(8):
        for which, extra in ((0, 0), (1, other)):
            idx = row_of(jnp.bitwise_xor(me, offs[n] ^ extra))
            yield n, which, pl.ds(pl.multiple_of(idx * rows, 16), rows)


def assemble(dst, keep, sent, me, offs, other, tile0, row_of):
    tiles, rows = keep.shape[1], keep.shape[2]
    for n, which, at in each_block(me, offs, other, rows, row_of):
        src = sent if which else keep
        for j in range(tiles):
            dst[at, pl.ds((tile0 + j) * LANES, LANES)] = src[n, j]


def disperse(src, keep, sent, me, offs, other, tile0, row_of):
    tiles, rows = keep.shape[1], keep.shape[2]
    for n, which, at in each_block(me, offs, other, rows, row_of):
        for j in range(tiles):
            value = src[at, pl.ds((tile0 + j) * LANES, LANES)]
            if which:
                sent[n, j] = value.astype(BF)
            else:
                keep[n, j] = value


def norm_kernel(scal, own, oth, cot, coth, gain, normed, normed_t, cot_all):
    me = scal[1]
    half = own.shape[0]
    mine = pl.ds(pl.multiple_of(me * half, half), half)
    theirs = pl.ds(pl.multiple_of((1 - me) * half, half), half)
    for at, ref in ((mine, own), (theirs, oth)):
        x = ref[...]
        r = lax.rsqrt(jnp.mean(x * x, axis=-1, keepdims=True) + EPS)
        normed[at, :] = (x * r * gain[...]).astype(BF)
    cot_all[mine, :] = cot[...].astype(BF)
    cot_all[theirs, :] = coth[...]
    normed_t[...] = normed[...].T


def lane_pick(a, p, lane):
    return jnp.where(lane < HEADDIM, a[:, 2 * p : 2 * p + 1], a[:, 2 * p + 1 : 2 * p + 2])


def softplus(v):
    return jnp.maximum(v, 0.0) + jnp.log1p(jnp.exp(-jnp.abs(v)))


def decays(raw, par):
    step = softplus(raw + par[0:1, :])
    rate = -jnp.exp(par[1:2, :])
    tri = (
        lax.broadcasted_iota(jnp.int32, (CHUNK, CHUNK), 0)
        >= lax.broadcasted_iota(jnp.int32, (CHUNK, CHUNK), 1)
    )
    log = mm(tri.astype(F32), rate * step, precision=BEST)
    return step, rate, log, tri


def scan_kernel(
    scal, normed, ka, sa, kb, sb, cw, par, skip, cols, rows,
    w1, proj, pre_o, mixed, states, xpad, state,
):
    me = scal[0]
    assemble(w1, ka, sa, me, OFF_A, 2, 0, in_row)
    assemble(w1, kb, sb, me, OFF_B, 1, TILES1A, in_row)
    xpad[pl.ds(0, 8), :] = jnp.zeros((8, XBC), F32)
    state[...] = jnp.zeros_like(state)

    def chunk(c, _):
        r0 = pl.multiple_of(c * CHUNK, CHUNK)
        at = pl.ds(r0, CHUNK)
        pj = mm(normed[at, :], w1[...]).astype(BF)
        proj[at, :] = pj
        xpad[pl.ds(r0 + 8, CHUNK), :] = pj[:, :XBC].astype(F32)
        col = cols[at, :]
        acts = []
        for t in range(XBC // LANES):
            ls = pl.ds(t * LANES, LANES)
            v = xpad[pl.ds(r0, CHUNK + 8), ls]
            total = cw[4:5, ls] + cw[3:4, ls] * v[8:]
            for j in (1, 2, 3):
                total = total + (col[:, j : j + 1] * cw[3 - j : 4 - j, ls]) * v[8 - j : CHUNK + 8 - j]
            pre_o[at, ls] = total
            acts.append(total * jax.nn.sigmoid(total))
        b_mat, c_mat = acts[PAIRS].astype(BF), acts[PAIRS + 1].astype(BF)
        step, _rate, log, tri = decays(pj[:, XBC:].astype(F32), par)
        log_t = log.T
        scores = nt(c_mat, b_mat)
        mask = tri & (col[:, 6:7] == rows[0:1, at])
        grow = jnp.exp(log) * col[:, 4:5]
        tail = jnp.exp(log[CHUNK - 1 :, :] - log) * col[:, 5:6]
        lane = lax.broadcasted_iota(jnp.int32, (CHUNK, LANES), 1)
        b_t = acts[PAIRS].T.astype(BF)
        states[c] = state[...]
        for p in range(PAIRS):
            ls = pl.ds(p * LANES, LANES)
            scaled = acts[p] * lane_pick(step, p, lane)
            low = jnp.where(lane < HEADDIM, scaled, 0.0)
            both = jnp.concatenate([low, scaled - low], axis=0).astype(BF)
            ws = []
            for h in (2 * p, 2 * p + 1):
                diff = log[:, h : h + 1] - log_t[h : h + 1, :]
                ws.append(scores * jnp.exp(jnp.where(mask, diff, -1e30)))
            y = mm(jnp.concatenate(ws, axis=1).astype(BF), both)
            old = state[:, ls]
            grown = lane_pick(grow, p, lane)
            y = y + mm(c_mat, old.astype(BF)) * grown
            mixed[at, ls] = y + skip[0:1, ls] * acts[p]
            ended = scaled * lane_pick(tail, p, lane)
            state[:, ls] = grown[CHUNK - 1 :, :] * old + mm(b_t, ended.astype(BF))
        return 0

    lax.fori_loop(0, normed.shape[0] // CHUNK, chunk, 0)


def gate_kernel(scal, normed, cot, kz, sz, ko, so, mixed, gg, wz, wo, z_o, dm_o, stats):
    me = scal[0]
    assemble(wz, kz, sz, me, OFF_A, 2, 0, in_row)
    assemble(wo, ko, so, me, OFF_B, 1, 0, out_row)

    def chunk(c, _):
        at = pl.ds(pl.multiple_of(c * CHUNK, CHUNK), CHUNK)
        zb = mm(normed[at, :], wz[...]).astype(BF)
        z_o[at, :] = zb
        z = zb.astype(F32)
        gated = mixed[at, :] * (z * jax.nn.sigmoid(z))
        dm = nt(cot[at, :], wo[...])
        dm_o[at, :] = dm
        first = jnp.sum(gated * gated, axis=1, keepdims=True)
        second = jnp.sum(dm * gg[...] * gated, axis=1, keepdims=True)
        lane = lax.broadcasted_iota(jnp.int32, (CHUNK, LANES), 1)
        stats[at, :] = jnp.where(lane == 0, first, second)
        return 0

    lax.fori_loop(0, normed.shape[0] // CHUNK, chunk, 0)


def gate_back_kernel(
    scal, mine, theirs, mixed, z_i, dm_i, gg, cot, normed_t,
    mixer, dz_o, dmixed, kz, sz, ko, so, grad,
):
    me = scal[0]

    def chunk(c, _):
        at = pl.ds(pl.multiple_of(c * CHUNK, CHUNK), CHUNK)
        tot = mine[at, :] + theirs[at, :]
        r = lax.rsqrt(tot[:, 0:1] * (1.0 / INNER) + EPS)
        s2 = tot[:, 1:2] * (1.0 / INNER)
        z = z_i[at, :].astype(F32)
        sig = jax.nn.sigmoid(z)
        act = z * sig
        mx = mixed[at, :]
        gated = mx * act
        dm = dm_i[at, :]
        mixer[at, :] = (gated * r * gg[...]).astype(BF)
        dg = r * (dm * gg[...]) - gated * (r * r * r * s2)
        dmixed[at, :] = dg * act
        dz_o[at, :] = (dg * mx * (sig * (1.0 + z * (1.0 - sig)))).astype(BF)
        return 0

    lax.fori_loop(0, mixed.shape[0] // CHUNK, chunk, 0)
    grad[...] = tn(mixer[...], cot[...])
    disperse(grad, ko, so, me, OFF_B, 1, 0, out_row)
    grad[...] = mm(normed_t[...], dz_o[...])
    disperse(grad, kz, sz, me, OFF_A, 2, 0, in_row)


def head_sum(value, ones):
    high = value.astype(BF)
    low = (value - high.astype(F32)).astype(BF)
    return mm(high, ones) + mm(low, ones)


def scan_back_kernel(
    dmixed, proj, pre_i, states, cw, par, skip, cols, rows,
    dproj, small, dpre, dstate, col_s, row_s, wide, wide2,
):
    count = dmixed.shape[0] // CHUNK
    length = dmixed.shape[0]
    dstate[...] = jnp.zeros_like(dstate)
    small[...] = jnp.zeros_like(small)
    col_s[...] = jnp.zeros_like(col_s)
    row_s[...] = jnp.zeros_like(row_s)
    dpre[pl.ds(length, 8), :] = jnp.zeros((8, XBC), F32)
    ones = (
        lax.broadcasted_iota(jnp.int32, (LOCAL, LANES), 0) // HEADDIM
        == lax.broadcasted_iota(jnp.int32, (LOCAL, LANES), 1)
    ).astype(BF)

    def chunk(k, _):
        c = count - 1 - k
        r0 = pl.multiple_of(c * CHUNK, CHUNK)
        at = pl.ds(r0, CHUNK)
        col = cols[at, :]
        acts, slopes = [], []
        for t in range(XBC // LANES):
            v = pre_i[at, pl.ds(t * LANES, LANES)]
            sig = jax.nn.sigmoid(v)
            acts.append(v * sig)
            slopes.append(sig * (1.0 + v * (1.0 - sig)))
        b_f, c_f = acts[PAIRS], acts[PAIRS + 1]
        b_mat, c_mat = b_f.astype(BF), c_f.astype(BF)
        c_t = c_f.T.astype(BF)
        raw = proj[at, pl.ds(XBC, LANES)].astype(F32)
        step, rate, log, tri = decays(raw, par)
        log_t = log.T
        scores = nt(c_mat, b_mat)
        row_i = lax.broadcasted_iota(jnp.int32, (CHUNK, CHUNK), 0)
        lane = lax.broadcasted_iota(jnp.int32, (CHUNK, LANES), 1)
        mask = tri & (col[:, 6:7] == rows[0:1, at])
        strict = row_i > lane
        grow = jnp.exp(log) * col[:, 4:5]
        tail = jnp.exp(log[CHUNK - 1 :, :] - log) * col[:, 5:6]
        d_scores = jnp.zeros((CHUNK, CHUNK), F32)
        d_b = jnp.zeros((CHUNK, NSTATE), F32)
        d_c = jnp.zeros((CHUNK, NSTATE), F32)
        ends, skips = [], []
        for p in range(PAIRS):
            ls = pl.ds(p * LANES, LANES)
            dy = dmixed[at, ls]
            val = acts[p]
            stepped = lane_pick(step, p, lane)
            scaled = val * stepped
            low = jnp.where(lane < HEADDIM, dy, 0.0)
            both = jnp.concatenate([low, dy - low], axis=0).astype(BF)
            d_w = nt(both, scaled.astype(BF))
            ws = []
            for q in range(2):
                h = 2 * p + q
                diff = log[:, h : h + 1] - log_t[h : h + 1, :]
                decay = jnp.exp(jnp.where(mask, diff, -1e30))
                w = scores * decay
                ws.append(w.astype(BF))
                part = d_w[q * CHUNK : (q + 1) * CHUNK]
                d_scores = d_scores + part * decay
                g = jnp.where(strict, part * w, 0.0)
                col_s[:, h : h + 1] = jnp.sum(g, axis=1, keepdims=True)
                row_s[h : h + 1, :] = jnp.sum(g, axis=0, keepdims=True)
            d_scaled = tn(jnp.concatenate(ws, axis=0), both)
            old = states[c, :, ls]
            old_bf = old.astype(BF)
            grown = lane_pick(grow, p, lane)
            d_cs = dy * grown
            d_cs_bf = d_cs.astype(BF)
            d_c = d_c + nt(d_cs_bf, old_bf)
            entered = d_cs * mm(c_mat, old_bf)
            later = dstate[:, ls]
            later_bf = later.astype(BF)
            tailed = lane_pick(tail, p, lane)
            ended = scaled * tailed
            d_ended = mm(b_mat, later_bf)
            d_b = d_b + nt(ended.astype(BF), later_bf)
            leaving = d_ended * ended
            d_scaled = d_scaled + d_ended * tailed
            through = grown[CHUNK - 1 :, :]
            ends.append(
                jnp.sum(leaving, axis=0, keepdims=True)
                + through * jnp.sum(later * old, axis=0, keepdims=True)
            )
            dstate[:, ls] = through * later + mm(c_t, d_cs_bf)
            wide[:, ls] = entered - leaving
            wide2[:, ls] = d_scaled * val
            skips.append(jnp.sum(dy * val, axis=0, keepdims=True))
            dpre[at, ls] = (d_scaled * stepped + skip[0:1, ls] * dy) * slopes[p]
        d_s = d_scores.astype(BF)
        d_c = d_c + mm(d_s, b_mat)
        d_b = d_b + tn(d_s, c_mat)
        dpre[at, pl.ds(LOCAL, LANES)] = d_b * slopes[PAIRS]
        dpre[at, pl.ds(LOCAL + LANES, LANES)] = d_c * slopes[PAIRS + 1]
        end_row = jnp.concatenate(ends, axis=1)
        skip_row = jnp.concatenate(skips, axis=1)
        pad = jnp.zeros((6, LOCAL), F32)
        rowsums = head_sum(jnp.concatenate([end_row, skip_row, pad], axis=0), ones)
        d_log = col_s[...] - row_s[...].T + head_sum(wide[...], ones)
        d_log = d_log + jnp.where(row_i == CHUNK - 1, rowsums[0:1, :], 0.0)
        upper = (row_i <= lane).astype(F32)
        d_rate = mm(upper, d_log, precision=BEST)
        d_step = head_sum(wide2[...], ones) + rate * d_rate
        d_raw = d_step * jax.nn.sigmoid(raw + par[0:1, :])
        d_raw = jnp.where(lane < 2 * PAIRS, d_raw, 0.0)
        dproj[at, pl.ds(XBC, LANES)] = d_raw.astype(BF)
        heads = pl.ds(0, LANES)
        small[8:9, heads] = small[8:9, heads] + jnp.sum(d_raw, axis=0, keepdims=True)
        small[9:10, heads] = small[9:10, heads] + jnp.sum(
            rate * step * d_rate, axis=0, keepdims=True
        )
        small[10:11, heads] = small[10:11, heads] + rowsums[1:2, :]
        return 0

    lax.fori_loop(0, count, chunk, 0)

    def taps(c, _):
        r0 = pl.multiple_of(c * CHUNK, CHUNK)
        at = pl.ds(r0, CHUNK)
        col = cols[pl.ds(r0, CHUNK + 8), :]
        for t in range(XBC // LANES):
            ls = pl.ds(t * LANES, LANES)
            x = proj[at, ls].astype(F32)
            d = dpre[pl.ds(r0, CHUNK + 8), ls]
            here = d[:CHUNK]
            total = cw[3:4, ls] * here
            sums = [jnp.sum(here * x, axis=0, keepdims=True)]
            for j in (1, 2, 3):
                moved = d[j : CHUNK + j] * col[j : CHUNK + j, j : j + 1]
                total = total + cw[3 - j : 4 - j, ls] * moved
                sums.append(jnp.sum(moved * x, axis=0, keepdims=True))
            dproj[at, ls] = total.astype(BF)
            bias = jnp.sum(here, axis=0, keepdims=True)
            new = jnp.concatenate(
                [sums[3], sums[2], sums[1], sums[0], bias, jnp.zeros((3, LANES), F32)], axis=0
            )
            small[0:8, ls] = small[0:8, ls] + new
        return 0

    lax.fori_loop(0, count, taps, 0)


def in_grad_kernel(scal, normed_t, dproj, ka, sa, kb, sb, grad):
    me = scal[0]
    grad[...] = mm(normed_t[...], dproj[...])
    disperse(grad, ka, sa, me, OFF_A, 2, 0, in_row)
    disperse(grad, kb, sb, me, OFF_B, 1, TILES1A, in_row)


def out_kernel(scal, mixer, wo, x, out, send):
    me = scal[1]
    half = x.shape[0]
    mine = pl.ds(pl.multiple_of(me * half, half), half)
    theirs = pl.ds(pl.multiple_of((1 - me) * half, half), half)
    send[...] = mm(mixer[theirs, :], wo[...]).astype(BF)
    out[...] = x[...] + mm(mixer[mine, :], wo[...])


def d_normed_kernel(scal, dz, dproj, wz, w1, own, send):
    me = scal[1]
    half = own.shape[0]
    mine = pl.ds(pl.multiple_of(me * half, half), half)
    theirs = pl.ds(pl.multiple_of((1 - me) * half, half), half)
    send[...] = (nt(dz[theirs, :], wz[...]) + nt(dproj[theirs, :], w1[...])).astype(BF)
    own[...] = nt(dz[mine, :], wz[...]) + nt(dproj[mine, :], w1[...])


def norm_back_kernel(own, came, x_i, gain, cot, out):
    x = x_i[...]
    r = lax.rsqrt(jnp.mean(x * x, axis=-1, keepdims=True) + EPS)
    d = (own[...] + came[...].astype(F32)) * gain[...]
    inner = jnp.mean(d * x, axis=-1, keepdims=True)
    out[...] = cot[...] + r * d - x * (r * r * r * inner)


def call(kernel, outs, args, name, scratch=(), smem=0, flops=0):
    vmem = pl.BlockSpec(memory_space=pltpu.VMEM)
    shapes = [jax.ShapeDtypeStruct(s, d) for s, d in outs]
    size = sum(int(a.size) * a.dtype.itemsize for a in args)
    size += sum(int(s.size) * s.dtype.itemsize for s in shapes)
    return pl.pallas_call(
        kernel,
        name=name,
        out_shape=shapes,
        in_specs=[pl.BlockSpec(memory_space=pltpu.SMEM)] * smem + [vmem] * (len(args) - smem),
        out_specs=[vmem] * len(shapes),
        scratch_shapes=list(scratch),
        compiler_params=pltpu.CompilerParams(vmem_limit_bytes=56 * 1024 * 1024),
        cost_estimate=pl.CostEstimate(flops=flops, bytes_accessed=size, transcendentals=0),
    )(*args)


def hop(value, bit):
    return lax.ppermute(value, "dp", [(i, i ^ bit) for i in range(BLOCKS)])


def core_swap(value):
    return lax.ppermute(value, "ctx", [(0, 1), (1, 0)])


def deal(value):
    pairs = []
    for z in range(4):
        for y in range(2):
            for x in range(2):
                for c in range(2):
                    pairs.append((2 * (4 * z + 2 * y + x) + c, 2 * (4 * z + 2 * c + x) + y))
    return lax.ppermute(value, ("dp", "ctx"), pairs)


def gather_blocks(mine, split):
    two = jnp.stack([mine, hop(mine, 8)])
    four = jnp.concatenate([two, hop(two, 4)])
    a, b = four[:, :split], four[:, split:]
    keep_a = jnp.concatenate([a, hop(a, 1)])
    keep_b = jnp.concatenate([b, hop(b, 2)])
    return keep_a, hop(keep_a, 2), keep_b, hop(keep_b, 1)


def scatter_blocks(keep_a, send_a, keep_b, send_b):
    came_a, came_b = hop(send_a, 2), hop(send_b, 1)
    more_a = hop((keep_a[4:] + came_a[4:]).astype(BF), 1)
    more_b = hop((keep_b[4:] + came_b[4:]).astype(BF), 2)
    four = jnp.concatenate(
        [keep_a[:4] + came_a[:4] + more_a, keep_b[:4] + came_b[:4] + more_b], axis=1
    )
    two = four[:2] + hop(four[2:].astype(BF), 4)
    return two[0] + hop(two[1].astype(BF), 8)


def flips(value, me):
    for axis in range(4):
        bit = (me >> (3 - axis)) & 1
        value = jnp.where(bit == 1, jnp.flip(value, axis), value)
    return value


def gather_small(mine, me):
    value = mine[None, None, None, None]
    for axis, bit in ((0, 8), (1, 4), (2, 2), (3, 1)):
        value = jnp.concatenate([value, hop(value, bit)], axis=axis)
    return flips(value, me).reshape((BLOCKS,) + mine.shape)


def scatter_small(full, me):
    value = flips(full.reshape((2, 2, 2, 2) + full.shape[1:]), me)
    for axis, bit in ((2, 2), (3, 1), (1, 4), (0, 8)):
        keep = lax.slice_in_dim(value, 0, 1, axis=axis)
        value = keep + hop(lax.slice_in_dim(value, 1, 2, axis=axis), bit)
    return value[0, 0, 0, 0]


def tiles_of(value):
    return jnp.swapaxes(value.reshape(value.shape[0], -1, LANES), 0, 1)


def flat_of(tiles):
    return jnp.swapaxes(tiles, 0, 1).reshape(tiles.shape[1], -1)


def by_core(value, axis):
    shape = value.shape
    rest = shape[axis] // (2 * SLABS)
    return value.reshape(shape[:axis] + (SLABS, 2, rest) + shape[axis + 1 :])


def core_part(value, axis, core):
    split = by_core(value, axis)
    part = lax.index_in_dim(split, core, axis + 1, keepdims=False)
    return part.reshape(value.shape[:axis] + (-1,) + value.shape[axis + 1 :])


def join_cores(own, came, axis, ctx):
    def split(v):
        shape = v.shape
        return v.reshape(shape[:axis] + (SLABS, shape[axis] // SLABS) + shape[axis + 1 :])

    first = jnp.where(ctx == 0, split(own), split(came))
    second = jnp.where(ctx == 0, split(came), split(own))
    both = jnp.stack([first, second], axis=axis + 1)
    return both.reshape(own.shape[:axis] + (-1,) + own.shape[axis + 1 :])


def choose(ctx, make):
    return jnp.where(ctx == 0, make(0), make(1))


def in_columns(weight, core):
    z = core_part(weight[:, :INNER], 1, core)
    x = core_part(weight[:, INNER : 2 * INNER], 1, core)
    bc = weight[:, 2 * INNER : INNER + CONVDIM]
    dt = core_part(weight[:, INNER + CONVDIM :], 1, core)
    dt = jnp.pad(dt, ((0, 0), (0, LANES - dt.shape[1])))
    return jnp.concatenate([x, bc, dt, z], axis=1)


def expected(me, offs, extra):
    return [o ^ extra for o in offs]


def shards(
    fast,
    inputs,
    segments,
    norm_gain,
    in_weight,
    conv_weight,
    conv_bias,
    dt_bias,
    a_log,
    d_skip,
    gate_gain,
    out_weight,
    cotangent,
):
    seq_count, half, width = inputs.shape
    assert seq_count == 1 and lax.axis_size("ctx") == 2
    length = 2 * half
    ctx = lax.axis_index("ctx").astype(jnp.int32)
    chip = lax.axis_index("dp").astype(jnp.int32) if fast else jnp.int32(0)
    scal = jnp.stack([chip, ctx])
    x_own, cot_own = inputs[0], cotangent[0]
    own_rows = in_weight.shape[0]

    if fast:
        for_me = choose(ctx, lambda k: in_columns(in_weight, k))
        for_other = choose(ctx, lambda k: in_columns(in_weight, 1 - k))
        came = core_swap(for_other)
        block = jnp.where(
            ctx == 0,
            jnp.concatenate([for_me, came]),
            jnp.concatenate([came, for_me]),
        )
        tiles = tiles_of(block)
        g1 = gather_blocks(tiles[:TILES1], TILES1A)
        g2 = gather_blocks(
            jnp.concatenate([tiles[TILES1:], tiles_of(deal(out_weight))]), TILESZ
        )
    else:
        in_full = lax.all_gather(in_weight, ("dp", "ctx"), axis=0, tiled=True)
        out_full = lax.all_gather(out_weight, ("dp", "ctx"), axis=0, tiled=True)
        mine = choose(ctx, lambda k: in_columns(in_full, k))
        tiles = jnp.swapaxes(tiles_of(mine).reshape(-1, BLOCKS, width // BLOCKS, LANES), 0, 1)
        rows_out = choose(ctx, lambda k: core_part(out_full, 0, k))
        tiles_out = jnp.swapaxes(tiles_of(rows_out).reshape(-1, BLOCKS, LOCAL // BLOCKS, LANES), 0, 1)
        order = jnp.array([out_row(i) for i in range(BLOCKS)])
        tiles_out = tiles_out[order]

        def arranged(v, offs, extra):
            return v[jnp.array(expected(0, offs, extra))]

        g1 = (
            arranged(tiles[:, :TILES1A], OFF_A, 0),
            arranged(tiles[:, :TILES1A], OFF_A, 2),
            arranged(tiles[:, TILES1A:TILES1], OFF_B, 0),
            arranged(tiles[:, TILES1A:TILES1], OFF_B, 1),
        )
        g2 = (
            arranged(tiles[:, TILES1:], OFF_A, 0),
            arranged(tiles[:, TILES1:], OFF_A, 2),
            arranged(tiles_out, OFF_B, 0),
            arranged(tiles_out, OFF_B, 1),
        )

    counts = (norm_gain.shape[0], conv_weight.size, conv_bias.shape[0], gate_gain.shape[0])
    packed = jnp.concatenate([norm_gain, conv_weight.reshape(-1), conv_bias, gate_gain])
    if fast:
        packed = jnp.pad(packed, (0, -packed.shape[0] % LANES)).reshape(-1, LANES)
        came = core_swap(packed)
        packed = jnp.where(ctx == 0, jnp.stack([packed, came]), jnp.stack([came, packed]))
        packed = gather_small(packed, chip).reshape(2 * BLOCKS, -1)
    else:
        packed = lax.all_gather(packed, ("dp", "ctx"), axis=0)
    parts, start = [], 0
    for count in counts:
        parts.append(packed[:, start : start + count].reshape(-1))
        start += count
    gain = parts[0].reshape(1, width)
    taps_all = parts[1].reshape(CONVDIM, CONV)
    conv_all = jnp.concatenate([taps_all, parts[2][:, None]], axis=1).T
    conv_mine = jnp.concatenate(
        [choose(ctx, lambda k: core_part(conv_all[:, :INNER], 1, k)), conv_all[:, INNER:]], axis=1
    )
    conv_mine = jnp.pad(conv_mine, ((0, 3), (0, 0)))
    gg = choose(ctx, lambda k: core_part(parts[3], 0, k)).reshape(1, LOCAL)

    def heads_mine(v):
        return choose(ctx, lambda k: core_part(v, 0, k))

    par = jnp.stack([heads_mine(dt_bias), heads_mine(a_log)])
    par = jnp.pad(par, ((0, 6), (0, LANES - par.shape[1])))
    skip = jnp.repeat(heads_mine(d_skip), HEADDIM).reshape(1, LOCAL)

    seg = segments[0].astype(F32)
    columns = [jnp.zeros_like(seg)]
    for j in (1, 2, 3):
        before = jnp.concatenate([jnp.full((j,), -1.0, F32), seg[:-j]])
        columns.append((before == seg).astype(F32))
    chunks = seg.reshape(-1, CHUNK)
    before = jnp.concatenate([jnp.full((1,), -1.0, F32), chunks[:-1, -1]])
    columns.append((chunks == before[:, None]).astype(F32).reshape(-1))
    columns.append((chunks == chunks[:, -1:]).astype(F32).reshape(-1))
    columns.append(seg)
    cols = jnp.pad(jnp.stack(columns, axis=1), ((0, 8), (0, LANES - 7)))
    rows = jnp.pad(seg[None], ((0, 7), (0, 0)))

    x_oth = core_swap(x_own)
    cot_oth = core_swap(cot_own.astype(BF))
    normed, normed_t, cot_all = call(
        norm_kernel,
        [((length, width), BF), ((width, length), BF), ((length, width), BF)],
        (scal, x_own, x_oth, cot_own, cot_oth, gain),
        "norm",
        smem=1,
    )
    w1, proj, pre, mixed, states = call(
        scan_kernel,
        [
            ((width, COLS1), BF),
            ((length, COLS1), BF),
            ((length, XBC), F32),
            ((length, LOCAL), F32),
            ((length // CHUNK, NSTATE, LOCAL), F32),
        ],
        (scal, normed, *g1, conv_mine, par, skip, cols, rows),
        "scan",
        scratch=[pltpu.VMEM((length + 8, XBC), F32), pltpu.VMEM((NSTATE, LOCAL), F32)],
        smem=1,
        flops=10**10,
    )
    wz, wo, z, dm, stats = call(
        gate_kernel,
        [
            ((width, LOCAL), BF),
            ((LOCAL, width), BF),
            ((length, LOCAL), BF),
            ((length, LOCAL), F32),
            ((length, LANES), F32),
        ],
        (scal, normed, cot_all, *g2, mixed, gg),
        "gate",
        smem=1,
        flops=2 * 10**9,
    )
    stats_oth = core_swap(stats)
    rows_in, rows_out = width // BLOCKS, LOCAL // BLOCKS
    mixer, dz, dmixed, *h2 = call(
        gate_back_kernel,
        [
            ((length, LOCAL), BF),
            ((length, LOCAL), BF),
            ((length, LOCAL), F32),
            ((8, TILESZ, rows_in, LANES), F32),
            ((8, TILESZ, rows_in, LANES), BF),
            ((8, width // LANES, rows_out, LANES), F32),
            ((8, width // LANES, rows_out, LANES), BF),
        ],
        (scal, stats, stats_oth, mixed, z, dm, gg, cot_all, normed_t),
        "gate_back",
        scratch=[pltpu.VMEM((width, LOCAL), F32)],
        smem=1,
        flops=2 * 10**9,
    )
    dproj, small = call(
        scan_back_kernel,
        [((length, COLS1), BF), ((16, XBC), F32)],
        (dmixed, proj, pre, states, conv_mine, par, skip, cols, rows),
        "scan_back",
        scratch=[
            pltpu.VMEM((length + 8, XBC), F32),
            pltpu.VMEM((NSTATE, LOCAL), F32),
            pltpu.VMEM((CHUNK, LANES), F32),
            pltpu.VMEM((LANES, CHUNK), F32),
            pltpu.VMEM((CHUNK, LOCAL), F32),
            pltpu.VMEM((CHUNK, LOCAL), F32),
        ],
        flops=10**10,
    )
    h1 = call(
        in_grad_kernel,
        [
            ((8, TILES1A, rows_in, LANES), F32),
            ((8, TILES1A, rows_in, LANES), BF),
            ((8, TILES1 - TILES1A, rows_in, LANES), F32),
            ((8, TILES1 - TILES1A, rows_in, LANES), BF),
        ],
        (scal, normed_t, dproj),
        "in_grad",
        scratch=[pltpu.VMEM((width, COLS1), F32)],
        smem=1,
        flops=10**9,
    )
    out_own, out_send = call(
        out_kernel,
        [((half, width), F32), ((half, width), BF)],
        (scal, mixer, wo, x_own),
        "out",
        smem=1,
        flops=6 * 10**8,
    )
    output = out_own + core_swap(out_send).astype(F32)
    dn_own, dn_send = call(
        d_normed_kernel,
        [((half, width), F32), ((half, width), BF)],
        (scal, dz, dproj, wz, w1),
        "d_normed",
        smem=1,
        flops=2 * 10**9,
    )
    (d_inputs,) = call(
        norm_back_kernel,
        [((half, width), F32)],
        (dn_own, core_swap(dn_send), x_own, gain, cot_own),
        "norm_back",
    )

    conv_x = small[:5, :LOCAL]
    zero = jnp.zeros_like(conv_x)
    conv_full = jnp.concatenate(
        [join_cores(conv_x, zero, 1, ctx), small[:5, LOCAL:]], axis=1
    ).T
    heads = small[8:11, : HEADS // 2]
    heads_full = join_cores(heads, jnp.zeros_like(heads), 1, ctx).reshape(-1)
    devices = lax.axis_size("dp") * 2
    share = conv_full.reshape(devices, -1)
    share = jnp.concatenate(
        [share, jnp.broadcast_to(heads_full, (devices, heads_full.shape[0]))], axis=1
    )

    if fast:
        share = jnp.pad(share, ((0, 0), (0, -share.shape[1] % LANES)))
        share = scatter_small(share.reshape(BLOCKS, 2, -1, LANES), chip)
        mine = lax.dynamic_index_in_dim(share, ctx, 0, keepdims=False)
        share = mine + core_swap(lax.dynamic_index_in_dim(share, 1 - ctx, 0, keepdims=False))
        share = share.reshape(-1)

        r2 = scatter_blocks(*h2)
        grad_out = flat_of(deal(r2[TILESZ:]))
        r1 = scatter_blocks(*h1)
        both = jnp.concatenate([r1, r2[:TILESZ]])
        mine = lax.dynamic_slice_in_dim(both, ctx * own_rows, own_rows, 1)
        came = core_swap(lax.dynamic_slice_in_dim(both, (1 - ctx) * own_rows, own_rows, 1))
        mine, came = flat_of(mine), flat_of(came)
        grad_in = jnp.concatenate(
            [
                join_cores(mine[:, COLS1:], came[:, COLS1:], 1, ctx),
                join_cores(mine[:, :LOCAL], came[:, :LOCAL], 1, ctx),
                mine[:, LOCAL:XBC] + came[:, LOCAL:XBC],
                join_cores(
                    mine[:, XBC : XBC + HEADS // 2], came[:, XBC : XBC + HEADS // 2], 1, ctx
                ),
            ],
            axis=1,
        )
    else:
        share = lax.psum_scatter(share, ("dp", "ctx"), scatter_dimension=0, tiled=True).reshape(-1)

        def whole(keep, sent, offs, extra, row_of):
            blocks = [None] * BLOCKS
            for n in range(8):
                blocks[row_of(offs[n])] = keep[n]
                blocks[row_of(offs[n] ^ extra)] = sent[n].astype(F32)
            full = jnp.stack(blocks)
            return jnp.swapaxes(full, 1, 2).reshape(BLOCKS * full.shape[2], -1)

        full_1 = jnp.concatenate(
            [whole(h1[0], h1[1], OFF_A, 2, in_row), whole(h1[2], h1[3], OFF_B, 1, in_row)], axis=1
        )
        full_z = whole(h2[0], h2[1], OFF_A, 2, in_row)
        full_o = whole(h2[2], h2[3], OFF_B, 1, out_row)
        nil_z = jnp.zeros_like(full_z)
        full_in = jnp.concatenate(
            [
                join_cores(full_z, nil_z, 1, ctx),
                join_cores(full_1[:, :LOCAL], nil_z, 1, ctx),
                full_1[:, LOCAL:XBC],
                join_cores(
                    full_1[:, XBC : XBC + HEADS // 2],
                    jnp.zeros_like(full_1[:, XBC : XBC + HEADS // 2]),
                    1,
                    ctx,
                ),
            ],
            axis=1,
        )
        full_out = join_cores(full_o, jnp.zeros_like(full_o), 0, ctx)
        grad_in = lax.psum_scatter(full_in, ("dp", "ctx"), scatter_dimension=0, tiled=True)
        grad_out = lax.psum_scatter(full_out, ("dp", "ctx"), scatter_dimension=0, tiled=True)

    own_channels = conv_bias.shape[0]
    conv_own = share[: own_channels * 5].reshape(own_channels, 5)
    heads_sum = share[own_channels * 5 : own_channels * 5 + 3 * HEADS].reshape(3, HEADS)
    grad_gain = jnp.sum(in_weight.astype(F32) * grad_in, axis=1) / norm_gain
    grad_gg = jnp.sum(out_weight.astype(F32) * grad_out, axis=1) / gate_gain
    return (
        output[None],
        d_inputs[None],
        grad_gain,
        grad_in,
        conv_own[:, :CONV],
        conv_own[:, CONV],
        heads_sum[0],
        heads_sum[1],
        heads_sum[2],
        grad_gg,
        grad_out,
    )


def solution(mesh):
    both = ("dp", "ctx")
    tokens, row, mat = P("dp", "ctx", None), P(both), P(both, None)
    fast = mesh.shape["dp"] == BLOCKS and mesh.shape["ctx"] == 2
    return jax.shard_map(
        functools.partial(shards, fast),
        mesh=mesh,
        in_specs=(tokens, P("dp", None), row, mat, mat, row, P(), P(), P(), row, mat, tokens),
        out_specs=(tokens, tokens, row, mat, mat, row, P(), P(), P(), row, mat),
        check_vma=False,
    )
```
